128 devices in a mesh: ctx: 32 (over y, z, core), head: 4 (over x).
Axes of the slice: x: 4, y: 4, z: 4, core: 2. Of those that a mesh axis runs over, the one named last changes fastest.
Arguments:
- inputs: bfloat16 [32768, 8192], P('ctx', 'head'), may hold values from -0.375 to 0.375
- state_in: bfloat16 [32768, 128], P('ctx'), may hold values from -0.5 to 0.5
- state_out: bfloat16 [32768, 128], P('ctx'), may hold values from -0.5 to 0.5
- level_weight: float32 [16, 32768], P(None, 'ctx'), may hold values from 0.25 to 1.5
- cotangent: bfloat16 [32768, 8192], P('ctx', 'head'), may hold values from -0.375 to 0.375
Outputs:
- output: bfloat16 [32768, 8192], P('ctx', 'head')
- grad_inputs: bfloat16 [32768, 8192], P('ctx', 'head')
- grad_state_in: float32 [32768, 128], P('ctx')
- grad_state_out: float32 [32768, 128], P('ctx')
- grad_level_weight: float32 [16, 32768], P(None, 'ctx')
- state_adjoint: float32 [32, 128, 8192], P('ctx', None, 'head')
The draws below stay inside these ranges and needn't reach their ends.
All inputs are finite; a program needn't handle non-finite values.
Results may differ from the reference program's by a relative error of at most 0.0057.
Values sent between devices are 32-bit elements; how exact they have to be, the bound alone decides.
No kernel may reach another device: no remote copies, remote signals or barrier semaphores. Data moves between devices by JAX's collectives and lax.ppermute only.
A program may use at most 192 MiB of HBM per device.

```python
import jax
import jax.numpy as jnp
from jax import lax

HEADS = 128
HEAD_DIM = 64
N_STATE = 128
TOK = 1024
BLOCKS = 32
TOKENS = 32768
TOK_BITS = 10
CTX_BITS = 5
LEVELS = 16


def levels(rng, extent, shards, low, top_value):
    def one(dim, blocks):
        steps = jax.random.uniform(jax.random.fold_in(jax.random.fold_in(rng, 6), dim), (blocks,), jnp.float32, low / len(shards), top_value / len(shards))
        return jnp.repeat(jnp.exp(steps), extent[dim] // blocks).reshape((-1,) + (1,) * (len(extent) - dim - 1))

    level = one(*shards[0])
    for cut in shards[1:]:
        level = level * one(*cut)
    return level


def centred(rng, extent, spread, bound, cuts=(), kind=jnp.bfloat16):
    array = jax.random.normal(rng, extent, jnp.float32) * spread
    if len(cuts) > 0:
        array = levels(rng, extent, cuts, -0.22, 0.18) * array
    return jnp.clip(array, min=-bound, max=bound).astype(kind)


def setup_inputs(seed: int = 0) -> dict:
    streams_of = jax.random.split(jax.random.key(seed), 6)
    return {
        "inputs": centred(streams_of[0], (TOKENS, HEADS * HEAD_DIM), (TOKENS // N_STATE) ** -0.5, 0.375, ((0, 32), (1, 4))),
        "state_in": centred(streams_of[1], (TOKENS, N_STATE), N_STATE ** -0.5, 0.5, ((0, 32),)),
        "state_out": centred(streams_of[2], (TOKENS, N_STATE), N_STATE ** -0.5, 0.5, ((0, 32),)),
        "level_weight": jnp.clip(0.25 + 1.25 * jax.random.uniform(streams_of[3], (LEVELS, TOKENS), jnp.float32) ** levels(streams_of[3], (LEVELS, TOKENS), ((1, 32),), -0.2, 0.2), 0.25, 1.5),
        "cotangent": centred(streams_of[4], (TOKENS, HEADS * HEAD_DIM), (TOKENS // N_STATE) ** -0.5, 0.375, ((0, 32), (1, 4))),
    }


def level_table(rows, tok_bits):
    row_ids = lax.broadcasted_iota(jnp.int32, (rows, rows), 0)
    col_ids = lax.broadcasted_iota(jnp.int32, (rows, rows), 1)
    differ = jnp.bitwise_xor(row_ids, col_ids)
    level_map = jnp.zeros((rows, rows), jnp.int32)
    for bit_pos in range(tok_bits):
        level_map = level_map + (jnp.right_shift(differ, bit_pos) > 0).astype(jnp.int32)
    return level_map, col_ids <= row_ids


def intra_weights(level_rows, level_map, causal, tok_bits):
    weights = jnp.zeros(level_map.shape, jnp.float32)
    for level in range(tok_bits + 1):
        weights = jnp.where(level_map == level, level_rows[level][:, None], weights)
    return jnp.where(causal, weights, jnp.zeros_like(weights))


def contract_rows(left, right):
    return lax.dot_general(left, right, (((0,), (0,)), ((), ())), preferred_element_type=jnp.float32)


def contract_cols(left, right):
    return lax.dot_general(left, right, (((1,), (1,)), ((), ())), preferred_element_type=jnp.float32)


def reference(inputs, state_in, state_out, level_weight, cotangent):
    width = HEADS * HEAD_DIM
    x_blocks = inputs.reshape(BLOCKS, TOK, width)
    in_blocks = state_in.reshape(BLOCKS, TOK, N_STATE)
    out_blocks = state_out.reshape(BLOCKS, TOK, N_STATE)
    cot_blocks = cotangent.reshape(BLOCKS, TOK, width)
    lam_blocks = jnp.transpose(level_weight.reshape(LEVELS, BLOCKS, TOK), (1, 0, 2))
    block_ids = jnp.arange(BLOCKS, dtype=jnp.int32)

    def make_state(pair):
        return contract_rows(pair[0], pair[1])

    states = lax.map(make_state, (in_blocks, x_blocks))
    flat_states = states.reshape(BLOCKS, N_STATE * width)
    owner = block_ids[:, None]
    member = block_ids[None, :]
    out_float = out_blocks.astype(jnp.float32)
    buckets = []
    adjoint = jnp.zeros((BLOCKS, N_STATE * width), jnp.float32)
    for bit_pos in range(CTX_BITS):
        owner_bit = jnp.bitwise_and(jnp.right_shift(owner, bit_pos), 1)
        member_bit = jnp.bitwise_and(jnp.right_shift(member, bit_pos), 1)
        same_top = jnp.right_shift(owner, bit_pos + 1) == jnp.right_shift(member, bit_pos + 1)
        selector = ((owner_bit == 1) & (member_bit == 0) & same_top).astype(jnp.float32)
        bucket = jnp.dot(selector, flat_states, precision=lax.Precision.HIGHEST)
        buckets.append(bucket.astype(jnp.bfloat16).reshape(BLOCKS, N_STATE, width))
        has_bit = jnp.bitwise_and(jnp.right_shift(block_ids, bit_pos), 1).astype(jnp.float32)
        lam_rows = lam_blocks[:, TOK_BITS + 1 + bit_pos, :] * has_bit[:, None]
        scaled = (lam_rows[:, :, None] * out_float).astype(jnp.bfloat16)
        query = lax.map(make_state, (scaled, cot_blocks)).reshape(BLOCKS, N_STATE * width)
        adjoint = adjoint + jnp.dot(selector.T, query, precision=lax.Precision.HIGHEST)
    bucket_stack = jnp.stack(buckets, axis=1)
    adjoint = adjoint.reshape(BLOCKS, N_STATE, width)
    level_map, causal = level_table(TOK, TOK_BITS)

    def block_pass(pieces):
        x_b, in_b, out_b, cot_b, lam_b, bucket_b, adj_b = pieces
        gram_matrix = contract_cols(out_b, in_b)
        weights = intra_weights(lam_b, level_map, causal, TOK_BITS)
        mixing = (weights * gram_matrix).astype(jnp.bfloat16)
        total = jnp.dot(mixing, x_b, preferred_element_type=jnp.float32)
        out_f = out_b.astype(jnp.float32)
        grad_mix = contract_cols(cot_b, x_b)
        grad_gram = (weights * grad_mix).astype(jnp.bfloat16)
        product = jnp.where(causal, grad_mix * gram_matrix, jnp.zeros_like(grad_mix))
        level_grads = []
        for level in range(TOK_BITS + 1):
            level_grads.append(jnp.sum(jnp.where(level_map == level, product, jnp.zeros_like(product)), axis=1))
        grad_out = jnp.dot(grad_gram, in_b, preferred_element_type=jnp.float32)
        for bit_pos in range(CTX_BITS):
            lam_row = lam_b[TOK_BITS + 1 + bit_pos]
            total = total + lam_row[:, None] * jnp.dot(out_b, bucket_b[bit_pos], preferred_element_type=jnp.float32)
            pulled = contract_cols(cot_b, bucket_b[bit_pos])
            grad_out = grad_out + lam_row[:, None] * pulled
            level_grads.append(jnp.sum(out_f * pulled, axis=1))
        adj_bf = adj_b.astype(jnp.bfloat16)
        grad_in = contract_rows(grad_gram, out_b) + contract_cols(x_b, adj_bf)
        grad_x = contract_rows(mixing, cot_b) + jnp.dot(in_b, adj_bf, preferred_element_type=jnp.float32)
        return total.astype(jnp.bfloat16), grad_x.astype(jnp.bfloat16), grad_in, grad_out, jnp.stack(level_grads)

    output, grad_inputs, grad_in, grad_out, grad_level = lax.map(
        block_pass, (x_blocks, in_blocks, out_blocks, cot_blocks, lam_blocks, bucket_stack, adjoint))
    output = output.reshape(TOKENS, width)
    grad_inputs = grad_inputs.reshape(TOKENS, width)
    grad_in = grad_in.reshape(TOKENS, N_STATE)
    grad_out = grad_out.reshape(TOKENS, N_STATE)
    grad_level = jnp.transpose(grad_level, (1, 0, 2)).reshape(LEVELS, TOKENS)
    return output, grad_inputs, grad_in, grad_out, grad_level, adjoint
```

```python
import functools

import jax
import jax.numpy as jnp
from jax import lax
from jax.experimental import pallas as pl
from jax.experimental.pallas import tpu as pltpu
from jax.sharding import PartitionSpec as P


F32 = jnp.float32
BF16 = jnp.bfloat16
TOK = 1024
TOK_BITS = 10
NST = 128
CHUNKS = 2
TB = 256


def dot(a, b, ca=1, cb=0):
    return lax.dot_general(a, b, (((ca,), (cb,)), ((), ())), preferred_element_type=F32)


def flip(value):
    return value.astype(F32).T


def call(body, name, grid, in_specs, out_specs, out_shape, scratch, flops, nbytes, args):
    return pl.pallas_call(
        body,
        name=name,
        out_shape=out_shape,
        grid_spec=pltpu.PrefetchScalarGridSpec(
            num_scalar_prefetch=1,
            grid=grid,
            in_specs=in_specs,
            out_specs=out_specs,
            scratch_shapes=scratch,
        ),
        compiler_params=pltpu.CompilerParams(dimension_semantics=("arbitrary",) * len(grid)),
        cost_estimate=pl.CostEstimate(flops=flops, bytes_accessed=nbytes, transcendentals=0),
    )(*args)


def full(shape):
    return pl.BlockSpec(shape, lambda i, m: (0,) * len(shape))


def lam_bit(meta, lw, level):
    return lw[TOK_BITS + 1 + level : TOK_BITS + 2 + level, :] * meta[level].astype(F32)


def first_states(meta, x, g, b, c, lw, own, give, bt, qt):
    @pl.when(pl.program_id(0) == 0)
    def _():
        bt[...] = flip(b[...]).astype(BF16)
        qt[...] = (flip(c[...]) * lam_bit(meta, lw[...], 4)).astype(BF16)

    state = dot(bt[...], x[...])
    query = dot(qt[...], g[...])
    odd = meta[0] == 1
    own[...] = jnp.where(odd, query, state)
    give[...] = jnp.where(odd, state, query)


def other_queries(meta, g, c, lw, give, keep3, pair, scaled, ct_out, qt):
    @pl.when(pl.program_id(0) == 0)
    def _():
        ct = flip(c[...])
        ct_out[...] = ct.astype(BF16)
        for level in range(5):
            part = ct * lam_bit(meta, lw[...], level)
            if level < 4:
                qt[level * NST : (level + 1) * NST, :] = part.astype(BF16)
            scaled[:, level * NST : (level + 1) * NST] = part.T.astype(BF16)

    query = dot(qt[...], g[...])
    odd = meta[0] == 1
    q0 = query[:NST]
    q3 = query[3 * NST :]
    give[...] = jnp.where(odd, q0, q3)
    keep3[...] = q3
    pair[0] = query[2 * NST : 3 * NST]
    pair[1] = query[NST : 2 * NST]


def local_part(meta, x, g, b, c, lw, mix, mix_t, gi, go_t, lev):
    step = pl.program_id(0)

    @pl.when(step == 0)
    def _():
        gi[...] = jnp.zeros_like(gi)

    for row in range(TOK // TB):

        @pl.when(step == row)
        def _(row=row):
            size = (row + 1) * TB
            c_row = c[...]
            gm = dot(x[:size, :], g[...], 1, 1)
            gram = dot(b[:size, :], c_row, 1, 1)
            lev[...] = jnp.zeros_like(lev)
            for col in range(row + 1):
                at = slice(col * TB, (col + 1) * TB)
                gm_c = gm[at]
                gram_c = gram[at]
                if col < row:
                    level = 8 + (col ^ row).bit_length()
                    lam = lw[level : level + 1, :]
                    lev[level : level + 1, :] += jnp.sum(gm_c * gram_c, axis=0, keepdims=True)
                    w_mix = lam * gram_c
                    w_gm = lam * gm_c
                else:
                    s_id = lax.broadcasted_iota(jnp.int32, (TB, TB), 0)
                    t_id = lax.broadcasted_iota(jnp.int32, (TB, TB), 1)
                    differ = jnp.bitwise_xor(s_id, t_id)
                    causal = s_id <= t_id
                    product = jnp.where(causal, gm_c * gram_c, 0.0)
                    lam = jnp.broadcast_to(lw[8:9, :], (TB, TB))
                    for level in range(7, -1, -1):
                        lam = jnp.where(differ < 2**level, lw[level : level + 1, :], lam)
                    lam = jnp.where(causal, lam, 0.0)
                    for level in range(9):
                        inside = differ < 2**level
                        if level > 0:
                            inside = jnp.logical_and(inside, differ >= 2 ** (level - 1))
                        lev[level : level + 1, :] = jnp.sum(
                            jnp.where(inside, product, 0.0), axis=0, keepdims=True
                        )
                    w_mix = lam * gram_c
                    w_gm = lam * gm_c
                w_gm = w_gm.astype(BF16)
                mix_t[at, :] = w_mix.astype(BF16)
                mix[:, at] = w_mix.T.astype(BF16)
                gi[at, :] += dot(w_gm, c_row)
                part = dot(b[at, :], w_gm, 0, 0)
                if col == 0:
                    go_t[...] = part
                else:
                    go_t[...] += part


def pull(meta, bk, g, ct, lw, levels, go_t):
    parts = dot(bk[...], g[...], 1, 1)
    rows = []
    for i, level in enumerate(levels):
        pulled = parts[i * NST : (i + 1) * NST]
        go_t = go_t + lam_bit(meta, lw, level) * pulled
        rows.append(jnp.sum(ct * pulled, axis=0, keepdims=True) * meta[level].astype(F32))
    return go_t, rows


def settle(meta, bk, passed, arrived, place, k):
    width = passed.shape[1]
    value = jnp.where(meta[0] == 1, passed[...], arrived[...])
    bk[place * NST : (place + 1) * NST, k * width : (k + 1) * width] = value.astype(BF16)


def mid_pull(levels, meta, *refs):
    n = CHUNKS
    count = 2 * n * len(levels)
    g, ct, lw, go_in, lev_in, bk, go_out, lev_out = refs[count:]

    @pl.when(pl.program_id(0) == 0)
    def _():
        for i in range(count // 2):
            settle(meta, bk, refs[2 * i], refs[2 * i + 1], i // n, i % n)

    go_t, rows = pull(meta, bk, g, ct[...].astype(F32), lw[...], levels, go_in[...])
    go_out[...] = go_t
    lev_out[...] = lev_in[...]
    for level, row in zip(levels, rows):
        lev_out[TOK_BITS + 1 + level : TOK_BITS + 2 + level, :] = row


def tail_pull(levels, meta, *refs):
    n = CHUNKS
    count = 2 * n * len(levels)
    base = refs[count : count + n]
    g, x, ct, lw, gi_in, go_in, lev_in, out, bk, adj, adj_bf = refs[count + n :]

    @pl.when(pl.program_id(0) == 0)
    def _():
        for i in range(count // 2):
            settle(meta, bk, refs[2 * i], refs[2 * i + 1], i // n, i % n)
        for k in range(n):
            passed, last = refs[count - 2 * n + 2 * k], refs[count - 2 * n + 2 * k + 1]
            width = passed.shape[1]
            value = jnp.where(meta[0] == 1, last[...], passed[...] + base[k][...])
            adj[0, :, k * width : (k + 1) * width] = value
            adj_bf[:, k * width : (k + 1) * width] = value.astype(BF16)

    go_t, rows = pull(meta, bk, g, ct[...].astype(F32), lw[...], levels, go_in[...])
    out[0, :TB, :] = gi_in[...] + dot(x[...], adj_bf[...], 1, 1)
    out[0, TB : 2 * TB, :] = go_t.T
    lev = jnp.concatenate([lev_in[: TOK_BITS + 1 + levels[0], :]] + rows, axis=0)
    for half in range(2):
        at = 2 * TB + 16 * half
        out[0, at : at + 16, :] = lev[:, half * 128 : (half + 1) * 128]


def make_output(meta, mix, x, scaled, *refs):
    bk, out = refs[:-1], refs[-1]
    buckets = jnp.concatenate([r[...] for r in bk], axis=0)
    for row in range(TOK // TB):
        at = slice(row * TB, (row + 1) * TB)
        size = (row + 1) * TB
        total = dot(mix[at, :size], x[:size, :]) + dot(scaled[at, :], buckets)
        out[at, :] = total.astype(BF16)


def make_grad_inputs(meta, mix_t, g, b, adj_bf, out):
    for col in range(TOK // TB):
        at = slice(col * TB, (col + 1) * TB)
        total = dot(mix_t[at, col * TB :], g[col * TB :, :]) + dot(b[at, :], adj_bf[...])
        out[at, :] = total.astype(BF16)


def unpack(meta, r0, r1, r2, r3, gi, go, lev):
    source = pl.program_id(0)
    slot = lax.rem(meta[5] - source + 4, 4)
    for i, ref in enumerate((r0, r1, r2, r3)):

        @pl.when(slot == i)
        def _(ref=ref):
            gi[...] = ref[:TB, :]
            go[...] = ref[TB : 2 * TB, :]
            lev[:, :128] = ref[2 * TB : 2 * TB + 16, :]
            lev[:, 128:] = ref[2 * TB + 16 :, :]


def core(i):
    return i ^ 1


def z_low(i):
    return i ^ 2


def z_ref(i):
    return i ^ 6


def y_low(i):
    return i ^ 8


def y_ref(i):
    return i ^ 24


def sds(shape, dtype):
    return jax.ShapeDtypeStruct(shape, dtype)


def shards(inputs, state_in, state_out, level_weight, cotangent):
    rows, cols = inputs.shape
    n = CHUNKS
    width = cols // n
    cb = min(width, 512)
    steps = width // cb
    blocks = lax.axis_size("ctx")
    heads = lax.axis_size("head")
    position = lax.axis_index("ctx")
    iota = lax.iota(jnp.int32, 8)
    meta = jnp.where(iota < 5, (position >> iota) & 1, lax.axis_index("head"))
    odd = (position & 1) == 1

    def swap(value, even_to=core, odd_to=core):
        pairs = []
        for i in range(blocks):
            to = even_to if i % 2 == 0 else odd_to
            if to is not None:
                pairs.append((i, to(i)))
        return lax.ppermute(value, "ctx", pairs)

    acc = sds((NST, width), F32)
    acc_spec = pl.BlockSpec((NST, cb), lambda i, m: (0, i))
    small = full((rows, NST))
    lw_full = full((16, rows))
    own, give = [], []
    for k in range(n):
        strip = pl.BlockSpec((rows, cb), lambda i, m, k=k: (0, k * steps + i))
        a, d = call(
            first_states,
            "first_states",
            (steps,),
            [strip, strip, small, small, lw_full],
            [acc_spec, acc_spec],
            [acc, acc],
            [pltpu.VMEM((NST, rows), BF16)] * 2,
            4 * NST * rows * width,
            8 * NST * width + 4 * rows * width,
            (meta, inputs, cotangent, state_in, state_out, level_weight),
        )
        own.append(a)
        give.append(d)
    got = [swap(v) for v in give]
    give2, keep3, pair = [], [], []
    for k in range(n):
        strip = pl.BlockSpec((rows, cb), lambda i, m, k=k: (0, k * steps + i))
        a, d, e, scaled, ct = call(
            other_queries,
            "other_queries",
            (steps,),
            [strip, small, lw_full],
            [
                acc_spec,
                acc_spec,
                pl.BlockSpec((2, NST, cb), lambda i, m: (0, 0, i)),
                full((rows, 5 * NST)),
                full((NST, rows)),
            ],
            [acc, acc, sds((2, NST, width), F32), sds((rows, 5 * NST), BF16), sds((NST, rows), BF16)],
            [pltpu.VMEM((4 * NST, rows), BF16)],
            8 * NST * rows * width,
            16 * NST * width + 2 * rows * width,
            (meta, cotangent, state_out, level_weight),
        )
        give2.append(a)
        keep3.append(d)
        pair.append(e)

    send = [a + r for a, r in zip(own, got)]
    route = [(z_low, y_ref), (z_ref, y_low), (y_low, z_ref), (y_ref, z_low)]
    held = [jnp.where(odd, 0.0, s) for s in send]
    got2 = [swap(v) for v in give2]
    got_pair = [swap(v, core, None) for v in pair]
    got0 = [swap(v, core, None) for v in own]
    extra = [
        [jnp.where(odd, keep3[k] + got2[k], 0.0) for k in range(n)],
        [jnp.where(odd, pair[k][0] + got_pair[k][0], 0.0) for k in range(n)],
        [jnp.where(odd, pair[k][1] + got_pair[k][1], 0.0) for k in range(n)],
    ]
    received = [[(v, v) for v in got0]]
    for step in range(4):
        arrived = [swap(s, *route[step]) for s in send]
        if step < 3:
            over = [swap(r, core, None) for r in arrived]
            received.append(list(zip(over, arrived)))
            send = [h + r + e for h, r, e in zip(held, arrived, extra[step])]
            held = [h + r for h, r in zip(held, arrived)]
    last = [jnp.where(odd, h + r, r) for h, r in zip(held, arrived)]
    received.append(list(zip([swap(v) for v in last], last)))

    mix, mix_t, gi, go_t, lev = call(
        local_part,
        "local_part",
        (rows // TB,),
        [
            full((rows, cols)),
            pl.BlockSpec((TB, cols), lambda i, m: (i, 0)),
            small,
            pl.BlockSpec((TB, NST), lambda i, m: (i, 0)),
            pl.BlockSpec((16, TB), lambda i, m: (0, i)),
        ],
        [
            pl.BlockSpec((TB, rows), lambda i, m: (i, 0)),
            pl.BlockSpec((rows, TB), lambda i, m: (0, i)),
            small,
            pl.BlockSpec((NST, TB), lambda i, m: (0, i)),
            pl.BlockSpec((16, TB), lambda i, m: (0, i)),
        ],
        [
            sds((rows, rows), BF16),
            sds((rows, rows), BF16),
            sds((rows, NST), F32),
            sds((NST, rows), F32),
            sds((16, rows), F32),
        ],
        [],
        int(1.25 * rows * rows * cols),
        4 * rows * cols + 6 * rows * rows,
        (meta, inputs, cotangent, state_in, state_out, level_weight),
    )

    t_cols = pl.BlockSpec((NST, TB), lambda i, m: (0, i))
    t_lev = pl.BlockSpec((16, TB), lambda i, m: (0, i))
    t_rows = pl.BlockSpec((TB, cols), lambda i, m: (i, 0))
    early = (0, 1, 2)
    late = (3, 4)
    half = full((NST, width))
    bk_early, go_t, lev = call(
        functools.partial(mid_pull, early),
        "mid_pull",
        (rows // TB,),
        [half] * (2 * n * len(early)) + [t_rows, t_cols, t_lev, t_cols, t_lev],
        [full((len(early) * NST, cols)), t_cols, t_lev],
        [sds((len(early) * NST, cols), BF16), sds((NST, rows), F32), sds((16, rows), F32)],
        [],
        2 * len(early) * NST * rows * cols,
        2 * rows * cols,
        (
            meta,
            *[v for k in early for two in received[k] for v in two],
            cotangent,
            ct,
            level_weight,
            go_t,
            lev,
        ),
    )
    quarter = 2 * TB + 32
    packed, bk_late, adjoint, adj_bf = call(
        functools.partial(tail_pull, late),
        "tail_pull",
        (rows // TB,),
        [half] * (2 * n * len(late) + n)
        + [t_rows, t_rows, t_cols, t_lev, pl.BlockSpec((TB, NST), lambda i, m: (i, 0)), t_cols, t_lev],
        [
            pl.BlockSpec((1, quarter, NST), lambda i, m: (lax.rem(i - m[5] + 4, 4), 0, 0)),
            full((len(late) * NST, cols)),
            full((1, NST, cols)),
            full((NST, cols)),
        ],
        [
            sds((heads, quarter, NST), F32),
            sds((len(late) * NST, cols), BF16),
            sds((1, NST, cols), F32),
            sds((NST, cols), BF16),
        ],
        [],
        6 * NST * rows * cols,
        4 * rows * cols,
        (
            meta,
            *[v for k in late for two in received[k] for v in two],
            *got2,
            cotangent,
            inputs,
            ct,
            level_weight,
            gi,
            go_t,
            lev,
        ),
    )

    def turn(value, by):
        return lax.ppermute(value, "head", [(i, (i + by) % heads) for i in range(heads)])

    summed = packed[0]
    for by in (1, 2, 3):
        summed = summed + turn(packed[by], by)
    spread = [summed] + [turn(summed, by) for by in (1, 2, 3)]

    cols_rows = pl.BlockSpec((rows, 512), lambda i, m: (0, i))
    output = call(
        make_output,
        "make_output",
        (cols // 512,),
        [full((rows, rows)), cols_rows, full((rows, 5 * NST))]
        + [pl.BlockSpec((len(k) * NST, 512), lambda i, m: (0, i)) for k in (early, late)],
        cols_rows,
        sds((rows, cols), BF16),
        [],
        int(1.25 * rows * rows * cols) + 10 * NST * rows * cols,
        4 * rows * cols + 2 * rows * rows,
        (meta, mix, inputs, scaled, bk_early, bk_late),
    )
    grad_inputs = call(
        make_grad_inputs,
        "make_grad_inputs",
        (cols // 512,),
        [full((rows, rows)), cols_rows, small, pl.BlockSpec((NST, 512), lambda i, m: (0, i))],
        cols_rows,
        sds((rows, cols), BF16),
        [],
        int(1.25 * rows * rows * cols) + 2 * NST * rows * cols,
        4 * rows * cols + 2 * rows * rows,
        (meta, mix_t, cotangent, state_in, adj_bf),
    )
    t_block = pl.BlockSpec((TB, NST), lambda i, m: (i, 0))
    grad_in, grad_out, grad_level = call(
        unpack,
        "unpack",
        (heads,),
        [full((quarter, NST))] * 4,
        [t_block, t_block, t_lev],
        [sds((rows, NST), F32), sds((rows, NST), F32), sds((16, rows), F32)],
        [],
        0,
        4 * rows * NST * 4,
        (meta, *spread),
    )
    return (output, grad_inputs, grad_in, grad_out, grad_level, adjoint)


def solution(mesh):
    in_specs = (P("ctx", "head"), P("ctx", None), P("ctx", None), P(None, "ctx"), P("ctx", "head"))
    out_specs = (
        P("ctx", "head"),
        P("ctx", "head"),
        P("ctx", None),
        P("ctx", None),
        P(None, "ctx"),
        P("ctx", None, "head"),
    )
    return jax.shard_map(shards, mesh=mesh, in_specs=in_specs, out_specs=out_specs, check_vma=False)
```
